32 devices in a mesh: rep: 8 (over z, x), tp: 4 (over y, core).
Axes of the slice: x: 2, y: 2, z: 4, core: 2. Of those that a mesh axis runs over, the one named last changes fastest.
Arguments:
- hidden: bfloat16 [8192, 14336], P('rep', 'tp'), may hold values from -6 to 6
- grad_out: bfloat16 [8192, 2048], P('rep'), may hold values from -6 to 6
- weight: bfloat16 [8, 14336, 2048], P('rep', 'tp'), may hold values from -0.125 to 0.125
- alive: int32 [8, 4], replicated, may hold values from 0 to 1, as said below
Outputs:
- grad_hidden: bfloat16 [8192, 14336], P('rep', 'tp')
- grad_weight: float32 [7168, 2048], P('tp', 'rep')
The draws below stay inside these ranges and needn't reach their ends.
Inputs may be any that keep to these rules, and one draw needn't show every extreme that they name: `alive`: exactly 2 replicas have exactly two zeros in their row; every other row is all ones.
All inputs are finite; a program needn't handle non-finite values.
Results may differ from the reference program's by a relative error of at most 0.001.
Values may be sent and summed in bfloat16 or wider, within the bound.
A program may use at most 128 MiB of HBM per device.

```python
import jax
import jax.numpy as jnp
from jax import lax

D = 2048
FF = 7168
TOK = 1024
SLOT = 3584
TOKENS = 8192
DEGRADED = 2
N_REP = 8
N_TP = 4


def draw_alive(key, part):
    key_rep = jax.random.fold_in(key, 11)
    key_dev = jax.random.fold_in(key, 23)
    order = jax.random.permutation(key_rep, N_REP)
    degraded = jnp.zeros((N_REP,), jnp.int32).at[order[:DEGRADED]].set(1)
    scores = jax.random.randint(key_dev, (N_REP, N_TP), 0, 1 << 20) * N_TP + jnp.arange(N_TP, dtype=jnp.int32)[None, :]
    ranks = jnp.argsort(jnp.argsort(scores, axis=1, stable=True), axis=1, stable=True)
    lost = (ranks < 2).astype(jnp.int32)
    return (1 - degraded[:, None] * lost).astype(jnp.int32)


def block_levels(stream_key, shape, split, low, high):
    factor_of, own = 1.0, jax.random.fold_in(stream_key, 6)
    for axis_at, shards_of in split:
        draws = jnp.exp(jax.random.uniform(jax.random.fold_in(own, axis_at), (shards_of,), jnp.float32, low / len(split), high / len(split)))
        factor_of = factor_of * jnp.repeat(draws, shape[axis_at] // shards_of).reshape([-1 if axis == axis_at else 1 for axis in range(len(shape))])
    return factor_of


def gaussian(stream_key, shape, scale, most, cuts=(), kind=jnp.bfloat16):
    drawn = scale * jax.random.normal(stream_key, shape, jnp.float32)
    if cuts:
        drawn = drawn * block_levels(stream_key, shape, cuts, -0.22, 0.18)
    return jnp.clip(drawn, -most, most).astype(kind)


def setup_inputs(seed: int = 0) -> dict:
    key_list = jax.random.split(jax.random.key(seed), 5)
    return {
        "hidden": gaussian(key_list[0], (TOKENS, N_TP * SLOT), 1.0, 6.0, ((0, 8), (1, 4))),
        "grad_out": gaussian(key_list[1], (TOKENS, D), 1.0, 6.0, ((0, 8),)),
        "weight": gaussian(key_list[2], (N_REP, N_TP * SLOT, D), D ** -0.5, 0.125, ((0, 8), (1, 4))),
        "alive": draw_alive(jax.random.fold_in(key_list[4], 71), 0),
    }


def reference(hidden, grad_out, weight, alive):
    def one_replica(carry_sum, replica):
        alive_row = alive[replica]
        live_count = jnp.sum(alive_row)
        slice_width = FF // live_count
        inclusive = jnp.cumsum(alive_row)
        tok_rows = lax.dynamic_slice_in_dim(grad_out, (replica * TOK).astype(jnp.int32), TOK, 0)
        hid_rows = lax.dynamic_slice_in_dim(hidden, (replica * TOK).astype(jnp.int32), TOK, 0)
        weights = weight[replica]
        columns = jnp.arange(N_TP * SLOT, dtype=jnp.int32)
        device_of = columns // SLOT
        within = columns % SLOT
        usable = (alive_row[device_of] == 1) & (within < slice_width)
        product = lax.dot_general(tok_rows, weights, (((1,), (1,)), ((), ())), preferred_element_type=jnp.float32)
        grad_rows = jnp.where(usable[None, :], product, 0.0).astype(jnp.bfloat16)
        units = jnp.arange(FF, dtype=jnp.int32)
        rank_of = units // slice_width
        holder = jnp.sum((inclusive[None, :] <= rank_of[:, None]).astype(jnp.int32), axis=1)
        source_col = (holder * SLOT + units - rank_of * slice_width).astype(jnp.int32)
        full = jnp.take(hid_rows, source_col, axis=1)
        partial_value = lax.dot_general(full, tok_rows, (((0,), (0,)), ((), ())), preferred_element_type=jnp.float32)
        return carry_sum + partial_value, grad_rows

    start = jnp.zeros((FF, D), jnp.float32)
    summed, grad_all = lax.scan(one_replica, start, jnp.arange(N_REP, dtype=jnp.int32))
    grad_hidden = grad_all.reshape(TOKENS, N_TP * SLOT)
    grad_weight = summed * (float(TOKENS) ** -0.5)
    return grad_hidden, grad_weight
```

```python
import itertools

import jax
import jax.numpy as jnp
from jax import lax
from jax.sharding import PartitionSpec as P

FF = 7168
LANES = 128
CHUNKS = 3
TOP = 60000.0


def possible_edges(count):
    common = FF // count
    edges = set()
    rows = [[1] * count]
    for lost in itertools.combinations(range(count), 2):
        rows.append([int(i not in lost) for i in range(count)])
    for row in rows:
        if not sum(row):
            continue
        width = FF // sum(row)
        rank = 0
        for i in range(count):
            if row[i]:
                low, high = rank * width, (rank + 1) * width
                for j in range(count):
                    if low < (j + 1) * common and j * common < high:
                        edges.add((i, j))
                rank += 1
    return edges


def rep_masks(count):
    masks, bit = [], 1
    while bit < count:
        masks.append(bit)
        bit *= 2
    if len(masks) >= 3:
        masks[2] |= masks[1]
    return masks


def swap(x, axis, mask):
    size = lax.axis_size(axis)
    return lax.ppermute(x, axis, [(i, i ^ mask) for i in range(size)])


def chunk_bounds(width, parts):
    unit = LANES if width % LANES == 0 else width // 7
    units = width // unit
    parts = min(parts, units)
    cuts = [units * k // parts * unit for k in range(parts + 1)]
    return list(zip(cuts[:-1], cuts[1:]))


def local(hidden, grad_out, weight, alive):
    replica = lax.axis_index("rep")
    tensor_index = lax.axis_index("tp")
    tensor_count = lax.axis_size("tp")
    replica_count = lax.axis_size("rep")
    slot_width = hidden.shape[1]
    common_width = FF // tensor_count
    features = grad_out.shape[1]
    owned = features // replica_count
    alive_row = lax.dynamic_slice_in_dim(alive, replica, 1, 0)[0]
    live_count = jnp.sum(alive_row)
    slice_width = FF // live_count
    live_rank = jnp.cumsum(alive_row) - alive_row
    self_alive = alive_row[tensor_index]
    self_rank = live_rank[tensor_index]
    edges = possible_edges(tensor_count)
    masks = rep_masks(replica_count)

    most = jnp.stack([jnp.max(jnp.abs(hidden)), jnp.max(jnp.abs(grad_out))]).astype(jnp.float32)
    most = jnp.broadcast_to(most[:, None], (2, LANES))
    for axis, list_of in (("tp", rep_masks(tensor_count)), ("rep", masks)):
        for mask in list_of:
            most = jnp.maximum(most, swap(most, axis, mask))
    tokens = float(replica_count * grad_out.shape[0])
    bound = jnp.maximum(most[0, 0] * most[1, 0], 1e-30) * tokens
    scale = TOP / bound

    padded = jnp.pad(hidden, ((0, 0), (slot_width, slot_width)))

    def part_for(receiver, low, high):
        offset_cols = common_width * receiver - self_rank * slice_width + low
        first_col = jnp.clip(offset_cols + slot_width, 0, 2 * slot_width)
        window = lax.dynamic_slice_in_dim(padded, first_col, high - low, 1)
        position = jnp.arange(high - low) + offset_cols
        wanted = (position >= 0) & (position < slice_width) & (self_alive == 1)
        return jnp.where(wanted[None, :], window, jnp.zeros((), jnp.bfloat16))

    def relative(order):
        blocks = []
        for place in range(replica_count):
            owner = replica
            for level, i in enumerate(order):
                if place >> (len(order) - 1 - level) & 1:
                    owner = owner ^ masks[i]
            blocks.append(lax.dynamic_slice_in_dim(grad_out, owner * owned, owned, 1))
        return jnp.concatenate(blocks, 1)

    levels = len(masks)
    orders = [[(k + i) % levels for i in range(levels)] for k in range(levels)]
    bounds = chunk_bounds(common_width, CHUNKS)
    ordered = {}
    for k in range(len(bounds)):
        if k % levels not in ordered:
            ordered[k % levels] = relative(orders[k % levels])

    commons = []
    for low, high in bounds:
        common = part_for(tensor_index, low, high)
        for offset in (-2, -1, 1, 2):
            pairs = [(i, i + offset) for i in range(tensor_count) if (i, i + offset) in edges]
            if pairs:
                common = common + lax.ppermute(part_for(tensor_index + offset, low, high), "tp", pairs)
        commons.append(common)

    def contract(common, other):
        return lax.dot_general(
            common, other, (((0,), (0,)), ((), ())), preferred_element_type=jnp.float32
        ) * scale

    sums = []
    for k, common in enumerate(commons):
        other = ordered[k % levels]
        half = features // 2
        sent = contract(common, other[:, half:]).astype(jnp.float16)
        kept = contract(common, other[:, :half])
        for level, i in enumerate(orders[k % levels]):
            kept = kept + swap(sent, "rep", masks[i]).astype(jnp.float32)
            half = kept.shape[1] // 2
            if level < levels - 1:
                sent = kept[:, half:].astype(jnp.float16)
                kept = kept[:, :half]
        sums.append(kept)

    product = lax.dot_general(
        grad_out, weight[0], (((1,), (1,)), ((), ())), preferred_element_type=jnp.float32
    )
    columns = jnp.arange(slot_width)
    usable = (columns < slice_width) & (self_alive == 1)
    grad_hidden = jnp.where(usable[None, :], product, 0.0).astype(jnp.bfloat16)
    return (grad_hidden, jnp.concatenate(sums, 0) * (bound * (tokens**-0.5 / TOP)))


def solution(mesh):
    return jax.shard_map(
        local,
        mesh=mesh,
        in_specs=(P("rep", "tp"), P("rep", None), P("rep", "tp", None), P()),
        out_specs=(P("rep", "tp"), P("tp", "rep")),
        check_vma=False,
    )
```

```python
import itertools

import jax
import jax.numpy as jnp
from jax import lax
from jax.sharding import PartitionSpec as P

FF = 7168
LANES = 128
SHARES = (5, 4, 3, 2)
TOP = 60000.0


def possible_edges(count):
    common = FF // count
    edges = set()
    rows = [[1] * count]
    for lost in itertools.combinations(range(count), 2):
        rows.append([int(i not in lost) for i in range(count)])
    for row in rows:
        if not sum(row):
            continue
        width = FF // sum(row)
        rank = 0
        for i in range(count):
            if row[i]:
                low, high = rank * width, (rank + 1) * width
                for j in range(count):
                    if low < (j + 1) * common and j * common < high:
                        edges.add((i, j))
                rank += 1
    return edges


def rep_masks(count):
    masks, bit = [], 1
    while bit < count:
        masks.append(bit)
        bit *= 2
    if len(masks) >= 3:
        masks[2] |= masks[1]
    return masks


def swap(x, axis, mask):
    size = lax.axis_size(axis)
    return lax.ppermute(x, axis, [(i, i ^ mask) for i in range(size)])


def chunk_bounds(width, shares):
    unit = LANES if width % LANES == 0 else width // 7
    units = width // unit
    cuts = sorted({units * sum(shares[:k]) // sum(shares) * unit for k in range(len(shares) + 1)})
    return list(zip(cuts[:-1], cuts[1:]))


def after(values, *earlier):
    return lax.optimization_barrier((values, earlier))[0]


def local(hidden, grad_out, weight, alive):
    replica = lax.axis_index("rep")
    tensor_index = lax.axis_index("tp")
    tensor_count = lax.axis_size("tp")
    replica_count = lax.axis_size("rep")
    slot_width = hidden.shape[1]
    common_width = FF // tensor_count
    features = grad_out.shape[1]
    owned = features // replica_count
    alive_row = lax.dynamic_slice_in_dim(alive, replica, 1, 0)[0]
    live_count = jnp.sum(alive_row)
    slice_width = FF // live_count
    live_rank = jnp.cumsum(alive_row) - alive_row
    self_alive = alive_row[tensor_index]
    self_rank = live_rank[tensor_index]
    edges = possible_edges(tensor_count)
    masks = rep_masks(replica_count)

    most = jnp.stack([jnp.max(jnp.abs(hidden)), jnp.max(jnp.abs(grad_out))]).astype(jnp.float32)
    most = jnp.broadcast_to(most[:, None], (2, LANES))
    self_rank = after(self_rank, most)
    for axis, list_of in (("tp", rep_masks(tensor_count)[::-1]), ("rep", masks)):
        for mask in list_of:
            most = jnp.maximum(most, swap(most, axis, mask))
    tokens = float(replica_count * grad_out.shape[0])
    bound = jnp.maximum(most[0, 0] * most[1, 0], 1e-30) * tokens
    scale = TOP / bound

    padded = jnp.pad(hidden, ((0, 0), (slot_width, slot_width)))

    def part_for(receiver, low, high):
        offset_cols = common_width * receiver - self_rank * slice_width + low
        first_col = jnp.clip(offset_cols + slot_width, 0, 2 * slot_width)
        window = lax.dynamic_slice_in_dim(padded, first_col, high - low, 1)
        position = jnp.arange(high - low) + offset_cols
        wanted = (position >= 0) & (position < slice_width) & (self_alive == 1)
        return jnp.where(wanted[None, :], window, jnp.zeros((), jnp.bfloat16))

    def relative(order):
        blocks = []
        for place in range(replica_count):
            owner = replica
            for level, i in enumerate(order):
                if place >> (len(order) - 1 - level) & 1:
                    owner = owner ^ masks[i]
            blocks.append(lax.dynamic_slice_in_dim(grad_out, owner * owned, owned, 1))
        return jnp.concatenate(blocks, 1)

    levels = len(masks)
    orders = [[(k + i) % levels for i in range(levels)] for k in range(levels)]
    bounds = chunk_bounds(common_width, SHARES)
    ordered = {}
    for k in range(len(bounds)):
        if k % levels not in ordered:
            ordered[k % levels] = relative(orders[k % levels])

    offsets = []
    for offset in (-2, 2, -1, 1):
        pairs = [(i, i + offset) for i in range(tensor_count) if (i, i + offset) in edges]
        if pairs:
            offsets.append((offset, pairs))

    def pieces_of(k):
        return [part_for(tensor_index + offset, *bounds[k]) for offset, _ in offsets]

    def send(pieces):
        return [lax.ppermute(piece, "tp", pairs) for piece, (_, pairs) in zip(pieces, offsets)]

    def contract(common, other):
        return lax.dot_general(
            common, other, (((0,), (0,)), ((), ())), preferred_element_type=jnp.float32
        ) * scale

    def hidden_gradient(earlier):
        product = lax.dot_general(
            grad_out, weight[0], (((1,), (1,)), ((), ())), preferred_element_type=jnp.float32
        )
        columns = jnp.arange(slot_width)
        usable = (columns < after(slice_width, *earlier)) & (self_alive == 1)
        return jnp.where(usable[None, :], product, 0.0).astype(jnp.bfloat16)

    count = len(bounds)
    arrived = {k: send(pieces_of(k)) for k in range(min(2, count))}
    kept, received, earlier = {}, {}, ()
    grad_hidden = None
    for tick in range(count + levels - 1):
        for k in range(min(tick, count - 1), max(tick - levels, -1), -1):
            level = tick - k
            order = orders[k % levels]
            if level == 0:
                common = part_for(tensor_index, *bounds[k])
                for piece in after(arrived[k], *earlier):
                    common = common + piece
                other = ordered[k % levels]
                half = features // 2
                sent = contract(common, other[:, half:]).astype(jnp.float16)
                kept[k] = contract(common, other[:, :half])
                earlier = (sent,)
                if k + 2 < count:
                    pieces = after(pieces_of(k + 2), common)
                    arrived[k + 2] = send(pieces)
                    earlier += tuple(pieces)
            else:
                whole = kept[k] + after(received[k], *earlier).astype(jnp.float32)
                half = whole.shape[1] // 2
                sent = whole[:, half:].astype(jnp.float16)
                kept[k] = whole[:, :half]
                earlier = (sent,)
            received[k] = swap(sent, "rep", masks[order[level]])
            if grad_hidden is None:
                grad_hidden = hidden_gradient(earlier)
                earlier = (grad_hidden,)
    sums = [kept[k] + received[k].astype(jnp.float32) for k in range(count)]
    return (grad_hidden, jnp.concatenate(sums, 0) * (bound * (tokens**-0.5 / TOP)))


def solution(mesh):
    return jax.shard_map(
        local,
        mesh=mesh,
        in_specs=(P("rep", "tp"), P("rep", None), P("rep", "tp", None), P()),
        out_specs=(P("rep", "tp"), P("tp", "rep")),
        check_vma=False,
    )
```

```python
import itertools

import jax
import jax.numpy as jnp
from jax import lax
from jax.sharding import PartitionSpec as P

FF = 7168
LANES = 128
SHARES = (6, 5, 3)
TOP = 60000.0


def possible_edges(count):
    common = FF // count
    edges = set()
    rows = [[1] * count]
    for lost in itertools.combinations(range(count), 2):
        rows.append([int(i not in lost) for i in range(count)])
    for row in rows:
        if not sum(row):
            continue
        width = FF // sum(row)
        rank = 0
        for i in range(count):
            if row[i]:
                low, high = rank * width, (rank + 1) * width
                for j in range(count):
                    if low < (j + 1) * common and j * common < high:
                        edges.add((i, j))
                rank += 1
    return edges


def rounds_of(edges):
    rounds = []
    for i, j in sorted(edges, key=lambda edge: (edge[0] ^ edge[1], edge)):
        for one in rounds:
            if all(i != a and j != b for a, b in one):
                one.append((i, j))
                break
        else:
            rounds.append([(i, j)])
    return rounds[::-1]


def rep_masks(count):
    masks, bit = [], 1
    while bit < count:
        masks.append(bit)
        bit *= 2
    if len(masks) >= 3:
        masks[2] |= masks[1]
    return masks


def swap(x, axis, mask):
    size = lax.axis_size(axis)
    return lax.ppermute(x, axis, [(i, i ^ mask) for i in range(size)])


def chunk_bounds(width, shares):
    unit = LANES if width % LANES == 0 else width // 7
    units = width // unit
    cuts = sorted({units * sum(shares[:k]) // sum(shares) * unit for k in range(len(shares) + 1)})
    return list(zip(cuts[:-1], cuts[1:]))


def after(values, *earlier):
    return lax.optimization_barrier((values, earlier))[0]


def local(hidden, grad_out, weight, alive):
    replica = lax.axis_index("rep")
    tensor_index = lax.axis_index("tp")
    tensor_count = lax.axis_size("tp")
    replica_count = lax.axis_size("rep")
    slot_width = hidden.shape[1]
    common_width = FF // tensor_count
    features = grad_out.shape[1]
    owned = features // replica_count
    alive_row = lax.dynamic_slice_in_dim(alive, replica, 1, 0)[0]
    live_count = jnp.sum(alive_row)
    slice_width = FF // live_count
    live_rank = jnp.cumsum(alive_row) - alive_row
    self_alive = alive_row[tensor_index]
    self_rank = live_rank[tensor_index]
    edges = possible_edges(tensor_count)
    masks = rep_masks(replica_count)

    most = jnp.stack([jnp.max(jnp.abs(hidden)), jnp.max(jnp.abs(grad_out))]).astype(jnp.float32)
    most = jnp.broadcast_to(most[:, None], (2, LANES))
    self_rank = after(self_rank, most)
    for axis, list_of in (("tp", rep_masks(tensor_count)[::-1]), ("rep", masks)):
        for mask in list_of:
            most = jnp.maximum(most, swap(most, axis, mask))
    tokens = float(replica_count * grad_out.shape[0])
    bound = jnp.maximum(most[0, 0] * most[1, 0], 1e-30) * tokens
    scale = TOP / bound

    padded = jnp.pad(hidden, ((0, 0), (slot_width, slot_width)))

    def part_for(receiver, low, high):
        offset_cols = common_width * receiver - self_rank * slice_width + low
        first_col = jnp.clip(offset_cols + slot_width, 0, 2 * slot_width)
        window = lax.dynamic_slice_in_dim(padded, first_col, high - low, 1)
        position = jnp.arange(high - low) + offset_cols
        wanted = (position >= 0) & (position < slice_width) & (self_alive == 1)
        return jnp.where(wanted[None, :], window, jnp.zeros((), jnp.bfloat16))

    def relative(order):
        blocks = []
        for place in range(replica_count):
            owner = replica
            for level, i in enumerate(order):
                if place >> (len(order) - 1 - level) & 1:
                    owner = owner ^ masks[i]
            blocks.append(lax.dynamic_slice_in_dim(grad_out, owner * owned, owned, 1))
        return jnp.concatenate(blocks, 1)

    levels = len(masks)
    near = max(levels - 1, 1)
    orders = [[(k + i) % near for i in range(near)] + list(range(near, levels)) for k in range(near)]
    bounds = chunk_bounds(common_width, SHARES)
    ordered = {}
    for k in range(len(bounds)):
        if k % near not in ordered:
            ordered[k % near] = relative(orders[k % near])

    rounds = []
    for pairs in rounds_of((i, j) for i, j in edges if i != j):
        receivers = dict(pairs)
        table = jnp.array([receivers.get(i, i) for i in range(tensor_count)], jnp.int32)
        rounds.append((table[tensor_index], pairs))

    def pieces_of(k):
        return [part_for(receiver, *bounds[k]) for receiver, _ in rounds]

    def send(pieces):
        return [lax.ppermute(piece, "tp", pairs) for piece, (_, pairs) in zip(pieces, rounds)]

    def contract(common, other):
        return lax.dot_general(
            common, other, (((0,), (0,)), ((), ())), preferred_element_type=jnp.float32
        ) * scale

    def hidden_gradient(earlier):
        product = lax.dot_general(
            grad_out, weight[0], (((1,), (1,)), ((), ())), preferred_element_type=jnp.float32
        )
        columns = jnp.arange(slot_width)
        usable = (columns < after(slice_width, *earlier)) & (self_alive == 1)
        return jnp.where(usable[None, :], product, 0.0).astype(jnp.bfloat16)

    count = len(bounds)
    arrived = {k: send(pieces_of(k)) for k in range(min(2, count))}
    kept, received, earlier = {}, {}, ()
    grad_hidden = None
    for tick in range(count + levels - 1):
        for k in range(min(tick, count - 1), max(tick - levels, -1), -1):
            level = tick - k
            order = orders[k % near]
            if level == 0:
                common = part_for(tensor_index, *bounds[k])
                for piece in after(arrived[k], *earlier):
                    common = common + piece
                other = ordered[k % near]
                half = features // 2
                sent = contract(common, other[:, half:]).astype(jnp.float16)
                kept[k] = contract(common, other[:, :half])
                earlier = (sent,)
                if k + 2 < count:
                    pieces = after(pieces_of(k + 2), common)
                    arrived[k + 2] = send(pieces)
                    earlier += tuple(pieces)
            else:
                whole = kept[k] + after(received[k], *earlier).astype(jnp.float32)
                half = whole.shape[1] // 2
                sent = whole[:, half:].astype(jnp.float16)
                kept[k] = whole[:, :half]
                earlier = (sent,)
            received[k] = swap(sent, "rep", masks[order[level]])
            if grad_hidden is None:
                grad_hidden = hidden_gradient(earlier)
                earlier = (grad_hidden,)
    sums = [kept[k] + received[k].astype(jnp.float32) for k in range(count)]
    return (grad_hidden, jnp.concatenate(sums, 0) * (bound * (tokens**-0.5 / TOP)))


def solution(mesh):
    return jax.shard_map(
        local,
        mesh=mesh,
        in_specs=(P("rep", "tp"), P("rep", None), P("rep", "tp", None), P()),
        out_specs=(P("rep", "tp"), P("tp", "rep")),
        check_vma=False,
    )
```

```python
import itertools

import jax
import jax.numpy as jnp
from jax import lax
from jax.sharding import PartitionSpec as P

FF = 7168
LANES = 128
SHARES = (5, 5, 4)
TOP = 60000.0


def possible_edges(count):
    common = FF // count
    edges = set()
    rows = [[1] * count]
    for lost in itertools.combinations(range(count), 2):
        rows.append([int(i not in lost) for i in range(count)])
    for row in rows:
        if not sum(row):
            continue
        width = FF // sum(row)
        rank = 0
        for i in range(count):
            if row[i]:
                low, high = rank * width, (rank + 1) * width
                for j in range(count):
                    if low < (j + 1) * common and j * common < high:
                        edges.add((i, j))
                rank += 1
    return edges


def rounds_of(edges):
    rounds = []
    for i, j in sorted(edges, key=lambda edge: (edge[0] ^ edge[1], edge)):
        for one in rounds:
            if all(i != a and j != b for a, b in one):
                one.append((i, j))
                break
        else:
            rounds.append([(i, j)])
    return rounds[::-1]


def rep_masks(count):
    masks, bit = [], 1
    while bit < count:
        masks.append(bit)
        bit *= 2
    if len(masks) >= 3:
        masks[2] |= masks[1]
    return masks


def swap(x, axis, mask):
    size = lax.axis_size(axis)
    return lax.ppermute(x, axis, [(i, i ^ mask) for i in range(size)])


def chunk_bounds(width, shares):
    unit = LANES if width % LANES == 0 else width // 7
    units = width // unit
    cuts = sorted({units * sum(shares[:k]) // sum(shares) * unit for k in range(len(shares) + 1)})
    return list(zip(cuts[:-1], cuts[1:]))


def after(values, *earlier):
    return lax.optimization_barrier((values, earlier))[0]


def local(hidden, grad_out, weight, alive):
    replica = lax.axis_index("rep")
    tensor_index = lax.axis_index("tp")
    tensor_count = lax.axis_size("tp")
    replica_count = lax.axis_size("rep")
    slot_width = hidden.shape[1]
    common_width = FF // tensor_count
    features = grad_out.shape[1]
    owned = features // replica_count
    alive_row = lax.dynamic_slice_in_dim(alive, replica, 1, 0)[0]
    live_count = jnp.sum(alive_row)
    slice_width = FF // live_count
    live_rank = jnp.cumsum(alive_row) - alive_row
    self_alive = alive_row[tensor_index]
    self_rank = live_rank[tensor_index]
    edges = possible_edges(tensor_count)
    masks = rep_masks(replica_count)

    padded = jnp.pad(hidden, ((0, 0), (slot_width, slot_width)))

    def part_for(receiver, low, high):
        offset_cols = common_width * receiver - self_rank * slice_width + low
        first_col = jnp.clip(offset_cols + slot_width, 0, 2 * slot_width)
        window = lax.dynamic_slice_in_dim(padded, first_col, high - low, 1)
        position = jnp.arange(high - low) + offset_cols
        wanted = (position >= 0) & (position < slice_width) & (self_alive == 1)
        return jnp.where(wanted[None, :], window, jnp.zeros((), jnp.bfloat16))

    def relative(order):
        blocks = []
        for place in range(replica_count):
            owner = replica
            for level, i in enumerate(order):
                if place >> (len(order) - 1 - level) & 1:
                    owner = owner ^ masks[i]
            blocks.append(lax.dynamic_slice_in_dim(grad_out, owner * owned, owned, 1))
        return jnp.concatenate(blocks, 1)

    levels = len(masks)
    near = max(levels - 1, 1)
    orders = [[(k + i) % near for i in range(near)] + list(range(near, levels)) for k in range(near)]
    bounds = chunk_bounds(common_width, SHARES)
    ordered = {}
    for k in range(len(bounds)):
        if k % near not in ordered:
            ordered[k % near] = relative(orders[k % near])

    rounds = []
    for pairs in rounds_of((i, j) for i, j in edges if i != j):
        receivers = dict(pairs)
        table = jnp.array([receivers.get(i, i) for i in range(tensor_count)], jnp.int32)
        rounds.append((table[tensor_index], pairs))

    def pieces_of(k):
        return [part_for(receiver, *bounds[k]) for receiver, _ in rounds]

    def send(pieces):
        return [lax.ppermute(piece, "tp", pairs) for piece, (_, pairs) in zip(pieces, rounds)]

    first_pieces = pieces_of(0)

    seen = after((hidden, grad_out), *first_pieces)
    most = jnp.stack([jnp.max(jnp.abs(x)) for x in seen]).astype(jnp.float32)
    most = jnp.broadcast_to(most[:, None], (2, LANES))
    shared = most
    for axis, list_of in (("rep", masks), ("tp", rep_masks(tensor_count))):
        for mask in list_of:
            shared = most
            most = jnp.maximum(most, swap(most, axis, mask))
    tokens = float(replica_count * grad_out.shape[0])
    bound = jnp.maximum(most[0, 0] * most[1, 0], 1e-30) * tokens
    scale = TOP / bound

    def contract(common, other):
        return lax.dot_general(
            common, other, (((0,), (0,)), ((), ())), preferred_element_type=jnp.float32
        ) * scale

    def hidden_gradient(earlier):
        product = lax.dot_general(
            grad_out, weight[0], (((1,), (1,)), ((), ())), preferred_element_type=jnp.float32
        )
        columns = jnp.arange(slot_width)
        usable = (columns < after(slice_width, *earlier)) & (self_alive == 1)
        return jnp.where(usable[None, :], product, 0.0).astype(jnp.bfloat16)

    count = len(bounds)
    arrived = {0: send(first_pieces)}
    if count > 1:
        arrived[1] = send(after(pieces_of(1), shared))
    kept, received, earlier = {}, {}, ()
    grad_hidden = None
    for tick in range(count + levels - 1):
        for k in range(min(tick, count - 1), max(tick - levels, -1), -1):
            level = tick - k
            order = orders[k % near]
            if level == 0:
                common = part_for(tensor_index, *bounds[k])
                for piece in after(arrived[k], *earlier):
                    common = common + piece
                other = ordered[k % near]
                half = features // 2
                sent = contract(common, other[:, half:]).astype(jnp.float16)
                kept[k] = contract(common, other[:, :half])
                earlier = (sent,)
                if k + 2 < count:
                    pieces = after(pieces_of(k + 2), common)
                    arrived[k + 2] = send(pieces)
                    earlier += tuple(pieces)
            else:
                whole = kept[k] + after(received[k], *earlier).astype(jnp.float32)
                half = whole.shape[1] // 2
                sent = whole[:, half:].astype(jnp.float16)
                kept[k] = whole[:, :half]
                earlier = (sent,)
            received[k] = swap(sent, "rep", masks[order[level]])
            if grad_hidden is None:
                grad_hidden = hidden_gradient(earlier)
                earlier = (grad_hidden,)
    sums = [kept[k] + received[k].astype(jnp.float32) for k in range(count)]
    return (grad_hidden, jnp.concatenate(sums, 0) * (bound * (tokens**-0.5 / TOP)))


def solution(mesh):
    return jax.shard_map(
        local,
        mesh=mesh,
        in_specs=(P("rep", "tp"), P("rep", None), P("rep", "tp", None), P()),
        out_specs=(P("rep", "tp"), P("tp", "rep")),
        check_vma=False,
    )
```
